32 devices in a mesh: dp: 8 (over y, x, core), tensor: 4 (over z).
Axes of the slice: x: 2, y: 2, z: 4, core: 2. Of those that a mesh axis runs over, the one named last changes fastest.
Arguments:
- tokens: bfloat16 [4096, 3584], P('dp'), may hold values from -6 to 6
- gate_weight: bfloat16 [3584, 10240], P(None, 'tensor'), may hold values from -0.09375 to 0.09375
- up_act: bfloat16 [4096, 10240], P('dp', 'tensor'), may hold values from -6 to 6
- hidden_cot: bfloat16 [4096, 10240], P('dp', 'tensor'), may hold values from -6 to 6
- lag_grads: bfloat16 [8, 3584, 10240], P('dp', None, 'tensor'), may hold values from -8 to 8, as said below
- skip_mask: int32 [8], P('dp'), may hold values 0 or 1
- aggregate: float32 [3584, 10240], P('dp', 'tensor'), may hold values from -3 to 3
Outputs:
- new_aggregate: float32 [3584, 10240], P('dp', 'tensor')
- input_grad: bfloat16 [4096, 3584], P('dp', 'tensor')
- change_rms: float32 [8], P('dp')
The draws below stay inside these ranges and needn't reach their ends.
Inputs may be any that keep to these rules, and one draw needn't show every extreme that they name: `lag_grads`: real-valued.
All inputs are finite; a program needn't handle non-finite values. No bound on the sum of `skip_mask` on one device may be relied on, other than what follows from the above.
Results may differ from the reference program's by a relative error of at most 0.014.
Values may be sent and summed in bfloat16 or wider, within the bound.
A program may use at most 192 MiB of HBM per device.

```python
import jax
import jax.numpy as jnp
from jax import lax

D = 3584
FF = 10240
TOK_DEV = 512
TOKENS = 4096
N_DP = 8


def draw_lag_grads(key, part):
    keys = jax.random.split(jax.random.fold_in(key, 17), 4)
    worker = jnp.arange(N_DP).astype(jnp.float32)
    wscale = 0.03 * 10.0 ** ((worker + jax.random.uniform(keys[0], (N_DP,))) / N_DP)
    rowscale = jnp.exp(jax.random.uniform(keys[1], (D,)) * jnp.log(10.0))
    position = jnp.arange(FF).astype(jnp.float32) / FF
    colscale = jnp.exp(jax.random.uniform(keys[2], (FF,)) * jnp.log(10.0)) * 3.0 ** position
    noise = jnp.clip(jax.random.normal(keys[3], (N_DP, D, FF)), -5.0, 5.0)
    norm = 41.0
    values = noise * wscale[:, None, None] * rowscale[None, :, None] * colscale[None, None, :] / norm
    return jnp.clip(values, -8.0, 8.0).astype(jnp.bfloat16)


def plant(entries, own_key, smallest, high):
    place = [jax.random.randint(jax.random.fold_in(own_key, axis), (), 0, length) for axis, length in enumerate(entries.shape)]
    longest = entries.shape.index(max(entries.shape))
    beside = place[:longest] + [(place[longest] + 1) % entries.shape[longest]] + place[longest + 1:]
    return entries.at[tuple(place)].set(smallest).at[tuple(beside)].set(high)


def level_of(key, shape, cuts, least, top_value):
    def one(axis_at, parts):
        draws = jax.random.uniform(jax.random.fold_in(jax.random.fold_in(key, 6), axis_at), (parts,), jnp.float32, least / len(cuts), top_value / len(cuts))
        return jnp.repeat(jnp.exp(draws), shape[axis_at] // parts).reshape((-1,) + (1,) * (len(shape) - axis_at - 1))

    level = one(*cuts[0])
    for cut in cuts[1:]:
        level = level * one(*cut)
    return level


def centred(key, extent, scale, most, pieces=(), kind=jnp.bfloat16):
    gain = level_of(key, extent, pieces, -0.22, 0.18) if pieces else 1.0
    array = jax.random.normal(key, extent, jnp.float32) * scale * gain
    return jnp.minimum(jnp.maximum(array, -most), most).astype(kind)


def setup_inputs(seed: int = 0) -> dict:
    key_list = jax.random.split(jax.random.key(seed), 8)
    return {
        "tokens": centred(key_list[0], (TOKENS, D), 1.0, 6.0, ((0, 8),)),
        "gate_weight": centred(key_list[1], (D, FF), D ** -0.5, 0.09375, ((1, 4),)),
        "up_act": centred(key_list[2], (TOKENS, FF), 1.0, 6.0, ((0, 8), (1, 4))),
        "hidden_cot": centred(key_list[3], (TOKENS, FF), 1.0, 6.0, ((0, 8), (1, 4))),
        "lag_grads": draw_lag_grads(jax.random.fold_in(key_list[7], 71), 0),
        "skip_mask": plant((jax.random.randint(key_list[5], (N_DP,), 0, 2) < 1).astype(jnp.int32), jax.random.fold_in(key_list[5], 1), 0, 1),
        "aggregate": centred(key_list[6], (D, FF), 0.2, 3.0, ((0, 8), (1, 4)), jnp.float32),
    }


clip_level = 0.1

def reference(tokens, gate_weight, up_act, hidden_cot, lag_grads, skip_mask, aggregate):
    gate = jnp.dot(tokens, gate_weight, preferred_element_type=jnp.float32)
    sig = jax.nn.sigmoid(gate)
    d_gate = (hidden_cot.astype(jnp.float32) * up_act.astype(jnp.float32) * sig * (1.0 + gate * (1.0 - sig))).astype(jnp.bfloat16)
    input_grad = jnp.dot(d_gate, gate_weight.T, preferred_element_type=jnp.float32).astype(jnp.bfloat16)
    worker_tokens = tokens.reshape(N_DP, TOK_DEV, D)
    worker_dgate = d_gate.reshape(N_DP, TOK_DEV, FF)
    inverse = 1.0 / TOK_DEV

    def one_worker(total, item):
        x_rows, d_rows, lag, flag = item
        grad = lax.dot_general(x_rows, d_rows, (((0,), (0,)), ((), ())), preferred_element_type=jnp.float32) * inverse
        change = grad - lag.astype(jnp.float32)
        rms = jnp.sqrt(jnp.sum(change * change) / (D * FF) + 1e-06)
        factor = flag.astype(jnp.float32) * jnp.minimum(1.0, clip_level / rms)
        sent = (factor * change).astype(jnp.bfloat16).astype(jnp.float32)
        return (total + sent, rms)
    new_aggregate, change_rms = lax.scan(one_worker, aggregate, (worker_tokens, worker_dgate, lag_grads, skip_mask))
    return (new_aggregate, input_grad, change_rms)
```

```python
import functools

import jax
import jax.numpy as jnp
from jax import lax
from jax.experimental import pallas as pl
from jax.experimental.pallas import tpu as pltpu
from jax.sharding import PartitionSpec as P

MESH = pl.DeviceIdType.MESH
clip_level = 0.1
F32 = jnp.float32
BF16 = jnp.bfloat16


def pick(size, options):
    for option in options:
        if size % option == 0:
            return option
    return size


def kernel(cfg, x_ref, g_ref, mask_ref, lag_ref, w_ref, out_ref, ig_ref, rms_ref,
           xt, chg, r1, a1, a2, b1, b2, stream, pi, pir, acc, stat, statr,
           lsem, r1s, r1r, a1s, a1r, a2s, a2r, b1s, b1r, b2s, b2r, pis, pir_s, sts, strr):
    NX, NY, T, D, FF = cfg
    NC = NX * NY
    tok, F = g_ref.shape
    R = chg.shape[2]
    FH = F // 2
    CH = pi.shape[2]
    inverse = 1.0 / tok
    dp = lax.axis_index("dp")
    t = lax.axis_index("tensor")
    core = lax.rem(dp, 2)
    chip = dp // 2
    x = lax.rem(chip, NX)
    y = chip // NX

    def chip_at(xx, yy):
        return lax.rem(xx, NX) + NX * lax.rem(yy, NY)

    def peer(cc):
        return (2 * cc + core, t)

    partner = (2 * chip + 1 - core, t)

    barrier = pltpu.get_barrier_semaphore()
    peers = []
    for m in range(T):
        for c in range(2):
            if m or c:
                peers.append((2 * chip + (core if c == 0 else 1 - core), lax.rem(t + m, T)))
    for k in range(1, NX):
        peers.append(peer(chip_at(x + k, y)))
    for k in range(1, NY):
        peers.append(peer(chip_at(x, y + k)))
    for p in peers:
        pl.semaphore_signal(barrier, inc=1, device_id=p, device_id_type=MESH)

    def remote(src, dst, ss, rs, dev):
        return pltpu.make_async_remote_copy(
            src_ref=src, dst_ref=dst, send_sem=ss, recv_sem=rs, device_id=dev, device_id_type=MESH
        )

    def dest(i):
        own = i // NC
        cc = lax.rem(chip + 1 + lax.rem(i, NC), NC)
        par = own * core + (1 - own) * (1 - core)
        return cc, par

    def lag_copy(i):
        cc, par = dest(i)
        row = pl.multiple_of((2 * cc + par) * R, 8)
        slot = lax.rem(i, 2)
        return pltpu.make_async_copy(
            lag_ref.at[0, pl.ds(row, R), :], stream.at[slot, pl.ds(0, R), :], lsem.at[slot]
        )

    lag_copy(jnp.int32(0)).start()
    acc[...] = jnp.zeros_like(acc)
    XB = pick(D, (512, 256, 128))

    def transpose(k, _):
        o = pl.multiple_of(k * XB, XB)
        xt[pl.ds(o, XB), :] = x_ref[:, pl.ds(o, XB)].T
        return 0

    lax.fori_loop(0, D // XB, transpose, 0)
    pl.semaphore_wait(barrier, len(peers))

    NB = pick(F, (512, 256, 128))

    def r1_copy(cc):
        return remote(chg.at[cc, 1 - core], r1.at[cc], r1s.at[cc], r1r.at[cc], partner)

    def change_step(i, send, last):
        cc, par = dest(i)
        row = pl.multiple_of((2 * cc + par) * R, 8)
        slot = lax.rem(i, 2)
        if not last:
            lag_copy(i + 1).start()
        lag_copy(i).wait()
        left = xt[pl.ds(row, R), :]

        def tile(n, _):
            o = pl.multiple_of(n * NB, NB)
            g = jnp.dot(left, g_ref[:, pl.ds(o, NB)], preferred_element_type=F32) * inverse
            ch = g - stream[slot, pl.ds(0, R), pl.ds(o, NB)].astype(F32)
            acc[...] += (ch * ch).reshape(R // 8, 8, NB).sum(0)
            chg[cc, par, :, pl.ds(o, NB)] = ch.astype(BF16)
            return 0

        lax.fori_loop(0, F // NB, tile, 0)
        if send:
            r1_copy(cc).start()

    def send_step(i, _):
        change_step(i, True, False)
        return 0

    def own_step(i, _):
        change_step(i, False, False)
        return 0

    lax.fori_loop(0, NC, send_step, 0)
    lax.fori_loop(NC, 2 * NC - 1, own_step, 0)
    change_step(jnp.int32(2 * NC - 1), False, True)

    def w_copy(i):
        m, h = i // 2, lax.rem(i, 2)
        owner = lax.rem(t + 1 + m, T)
        row = pl.multiple_of(owner * (2 * CH) + h * CH, 8)
        return pltpu.make_async_copy(
            w_ref.at[pl.ds(row, CH), :], stream.at[h, pl.ds(0, CH), :], lsem.at[h]
        )

    w_copy(jnp.int32(0)).start()
    w_copy(jnp.int32(1)).start()

    total = jnp.sum(jnp.sum(acc[...], axis=1, keepdims=True), axis=0, keepdims=True)
    stat[0] = jnp.broadcast_to(total, (8, 128))
    stat[1] = jnp.full((8, 128), mask_ref[0].astype(F32), F32)
    stat_copies = []
    for m in range(T):
        for c in range(2):
            if m or c:
                n = 2 * m + c - 1
                stat_copies.append(remote(
                    stat, statr.at[n], sts.at[n], strr.at[n],
                    (2 * chip + (core if c == 0 else 1 - core), lax.rem(t + m, T))))
    for copy in stat_copies:
        copy.start()
    for copy in stat_copies:
        copy.wait()
    own_sq = stat[0]
    for m in range(1, T):
        own_sq = own_sq + statr[2 * m - 1, 0]
    par_sq = statr[0, 0]
    for m in range(1, T):
        par_sq = par_sq + statr[2 * m, 0]

    def rms_of(sq):
        return jnp.sqrt(sq / (D * FF) + 1e-06)

    rms_own = rms_of(own_sq)
    rms_ref[...] = rms_own
    f_own = (stat[1] * jnp.minimum(1.0, clip_level / rms_own))[0:1, 0:1]
    f_par = (statr[0, 1] * jnp.minimum(1.0, clip_level / rms_of(par_sq)))[0:1, 0:1]

    def r1_wait(cc, _):
        r1_copy(cc).wait()
        return 0

    lax.fori_loop(0, NC, r1_wait, 0)

    RB = pick(R, (64, 32, 16))

    def combine(cc, half, arrived, final):
        cols = pl.ds(half * FH, FH)

        def rows(i, _):
            rr = pl.ds(pl.multiple_of(i * RB, RB), RB)
            v = chg[cc, core, rr, cols].astype(F32) * f_own + r1[cc, rr, cols].astype(F32) * f_par
            for ref in arrived:
                v = v + ref[rr, :].astype(F32)
            if final:
                out_ref[rr, cols] = v.astype(BF16)
            else:
                chg[cc, core, rr, cols] = v.astype(BF16)
            return 0

        lax.fori_loop(0, R // RB, rows, 0)

    def half_of(cc, half):
        return chg.at[cc, core, :, pl.ds(half * FH, FH)]

    a1c, b1c, a2c, b2c = {}, {}, {}, {}

    def send_a1(k, j):
        cc = chip_at(x + k, y + j)
        combine(cc, 0, (), False)
        n = (k - 1) * NY + j
        a1c[k, j] = remote(half_of(cc, 0), a1.at[n], a1s.at[n], a1r.at[n], peer(chip_at(x + k, y)))
        a1c[k, j].start()

    def send_b1(k, j):
        cc = chip_at(x + j, y + k)
        combine(cc, 1, (), False)
        n = (k - 1) * NX + j
        b1c[k, j] = remote(half_of(cc, 1), b1.at[n], b1s.at[n], b1r.at[n], peer(chip_at(x, y + k)))
        b1c[k, j].start()

    order_a = [(k, j) for j in list(range(1, NY)) + [0] for k in range(1, NX)]
    order_b = [(k, j) for j in list(range(1, NX)) + [0] for k in range(1, NY)]
    for n in range(max(len(order_a), len(order_b))):
        if n < len(order_a):
            send_a1(*order_a[n])
        if n < len(order_b):
            send_b1(*order_b[n])

    def pi_copy(m, h):
        n = 2 * m + h
        return remote(pi.at[n], pir.at[n], pis.at[n], pir_s.at[n], (dp, lax.rem(t + 1 + m, T)))

    def pi_step(i, send, more):
        m, h = i // 2, lax.rem(i, 2)
        w_copy(i).wait()
        pi[i] = lax.dot_general(
            g_ref[...], stream[h, pl.ds(0, CH), :], (((1,), (1,)), ((), ())), preferred_element_type=F32
        ).astype(BF16)
        if more:
            w_copy(i + 2).start()
        if send:
            pi_copy(m, h).start()

    def pi_send(i, _):
        pi_step(i, True, True)
        return 0

    lax.fori_loop(0, 2 * (T - 1), pi_send, 0)

    def pi_own(i, _):
        pi_step(i, False, False)
        return 0

    lax.fori_loop(2 * (T - 1), 2 * T, pi_own, 0)

    for j in range(1, NY):
        for k in range(1, NX):
            a1c[k, j].wait()
        cc = chip_at(x, y + j)
        combine(cc, 0, [a1.at[(k - 1) * NY + j] for k in range(1, NX)], False)
        a2c[j] = remote(half_of(cc, 0), a2.at[j - 1], a2s.at[j - 1], a2r.at[j - 1], peer(cc))
        a2c[j].start()
    for j in range(1, NX):
        for k in range(1, NY):
            b1c[k, j].wait()
        cc = chip_at(x + j, y)
        combine(cc, 1, [b1.at[(k - 1) * NX + j] for k in range(1, NY)], False)
        b2c[j] = remote(half_of(cc, 1), b2.at[j - 1], b2s.at[j - 1], b2r.at[j - 1], peer(cc))
        b2c[j].start()

    for m in range(T - 1):
        for h in range(2):
            pi_copy(m, h).wait()
    TB = pick(tok, (64, 32, 16))
    for h in range(2):
        def ig_rows(i, _):
            rr = pl.ds(pl.multiple_of(i * TB, TB), TB)
            v = pi[2 * (T - 1) + h, rr, :].astype(F32)
            for m in range(T - 1):
                v = v + pir[2 * m + h, rr, :].astype(F32)
            ig_ref[rr, pl.ds(h * CH, CH)] = v.astype(BF16)
            return 0

        lax.fori_loop(0, tok // TB, ig_rows, 0)

    for k in range(1, NX):
        a1c[k, 0].wait()
    for j in range(1, NY):
        a2c[j].wait()
    combine(chip, 0, [a1.at[(k - 1) * NY] for k in range(1, NX)] + [a2.at[j - 1] for j in range(1, NY)], True)
    for k in range(1, NY):
        b1c[k, 0].wait()
    for j in range(1, NX):
        b2c[j].wait()
    combine(chip, 1, [b1.at[(k - 1) * NX] for k in range(1, NY)] + [b2.at[j - 1] for j in range(1, NX)], True)


def body(cfg, tokens, gate_weight, up_act, hidden_cot, lag_grads, skip_mask, aggregate):
    NX, NY, T, D, FF = cfg
    NC = NX * NY
    gate = jnp.dot(tokens, gate_weight, preferred_element_type=F32)
    sig = jax.nn.sigmoid(gate)
    d_gate = (
        hidden_cot.astype(F32) * up_act.astype(F32) * sig * (1.0 + gate * (1.0 - sig))
    ).astype(BF16)
    tok, F = d_gate.shape
    R = D // (2 * NC)
    CH = D // T // 2
    FH = F // 2
    NB = pick(F, (512, 256, 128))
    nA, nB = (NX - 1) * NY, (NY - 1) * NX
    vmem = pl.BlockSpec(memory_space=pltpu.VMEM)
    hbm = pl.BlockSpec(memory_space=pl.ANY)
    dma = pltpu.SemaphoreType.DMA
    summed, input_grad, rms = pl.pallas_call(
        functools.partial(kernel, cfg),
        out_shape=(
            jax.ShapeDtypeStruct((R, F), BF16),
            jax.ShapeDtypeStruct((tok, 2 * CH), BF16),
            jax.ShapeDtypeStruct((8, 128), F32),
        ),
        in_specs=[vmem, vmem, pl.BlockSpec(memory_space=pltpu.SMEM), hbm, hbm],
        out_specs=(vmem, vmem, vmem),
        scratch_shapes=[
            pltpu.VMEM((D, tok), BF16),
            pltpu.VMEM((NC, 2, R, F), BF16),
            pltpu.VMEM((NC, R, F), BF16),
            pltpu.VMEM((nA, R, FH), BF16),
            pltpu.VMEM((NY - 1, R, FH), BF16),
            pltpu.VMEM((nB, R, FH), BF16),
            pltpu.VMEM((NX - 1, R, FH), BF16),
            pltpu.VMEM((2, max(R, CH), F), BF16),
            pltpu.VMEM((2 * T, tok, CH), BF16),
            pltpu.VMEM((2 * (T - 1), tok, CH), BF16),
            pltpu.VMEM((8, NB), F32),
            pltpu.VMEM((2, 8, 128), F32),
            pltpu.VMEM((2 * T - 1, 2, 8, 128), F32),
            dma((2,)),
            dma((NC,)), dma((NC,)),
            dma((nA,)), dma((nA,)),
            dma((NY - 1,)), dma((NY - 1,)),
            dma((nB,)), dma((nB,)),
            dma((NX - 1,)), dma((NX - 1,)),
            dma((2 * (T - 1),)), dma((2 * (T - 1),)),
            dma((2 * T - 1,)), dma((2 * T - 1,)),
        ],
        compiler_params=pltpu.CompilerParams(
            collective_id=0, has_side_effects=True, vmem_limit_bytes=67043328
        ),
    )(tokens, d_gate, skip_mask, lag_grads, gate_weight)
    return (aggregate + summed.astype(F32), input_grad, rms[0, 0:1])


def solution(mesh):
    dp, tensor = mesh.shape["dp"], mesh.shape["tensor"]

    def whole(tokens, gate_weight, *rest):
        D, FF = gate_weight.shape
        cfg = (2, dp // 4, tensor, D, FF)
        return jax.shard_map(
            functools.partial(body, cfg),
            mesh=mesh,
            in_specs=(
                P("dp", None),
                P(None, "tensor"),
                P("dp", "tensor"),
                P("dp", "tensor"),
                P("dp", None, "tensor"),
                P("dp"),
                P("dp", "tensor"),
            ),
            out_specs=(P("dp", "tensor"), P("dp", "tensor"), P("dp")),
            check_vma=False,
        )(tokens, gate_weight, *rest)

    return whole
```

```python
import functools

import jax
import jax.numpy as jnp
from jax import lax
from jax.experimental import pallas as pl
from jax.experimental.pallas import tpu as pltpu
from jax.sharding import PartitionSpec as P

MESH = pl.DeviceIdType.MESH
clip_level = 0.1
F32 = jnp.float32
BF16 = jnp.bfloat16


def pick(size, options):
    for option in options:
        if size % option == 0:
            return option
    return size


def kernel(cfg, x_ref, g_ref, mask_ref, lag_ref, w_ref, out_ref, ig_ref, rms_ref,
           xt, chg, r1, a1, a2, b1, b2, stream, pi, zr, acc, stat, statr,
           lsem, r1s, r1r, a1s, a1r, a2s, a2r, b1s, b1r, b2s, b2r, zs, zrs, sts, strr):
    NX, NY, T, D, FF = cfg
    NC = NX * NY
    tok, F = g_ref.shape
    R = chg.shape[2]
    FH = F // 2
    CH = pi.shape[2]
    inverse = 1.0 / tok
    dp = lax.axis_index("dp")
    t = lax.axis_index("tensor")
    core = lax.rem(dp, 2)
    chip = dp // 2
    x = lax.rem(chip, NX)
    y = chip // NX

    def chip_at(xx, yy):
        return lax.rem(xx, NX) + NX * lax.rem(yy, NY)

    def peer(cc):
        return (2 * cc + core, t)

    partner = (2 * chip + 1 - core, t)

    barrier = pltpu.get_barrier_semaphore()
    peers = []
    for m in range(T):
        for c in range(2):
            if m or c:
                peers.append((2 * chip + (core if c == 0 else 1 - core), lax.rem(t + m, T)))
    for k in range(1, NX):
        peers.append(peer(chip_at(x + k, y)))
    for k in range(1, NY):
        peers.append(peer(chip_at(x, y + k)))
    for p in peers:
        pl.semaphore_signal(barrier, inc=1, device_id=p, device_id_type=MESH)

    def remote(src, dst, ss, rs, dev):
        return pltpu.make_async_remote_copy(
            src_ref=src, dst_ref=dst, send_sem=ss, recv_sem=rs, device_id=dev, device_id_type=MESH
        )

    def dest(i):
        own = i // NC
        cc = lax.rem(chip + 1 + lax.rem(i, NC), NC)
        par = own * core + (1 - own) * (1 - core)
        return cc, par

    def lag_copy(i):
        cc, par = dest(i)
        row = pl.multiple_of((2 * cc + par) * R, 8)
        slot = lax.rem(i, 2)
        return pltpu.make_async_copy(
            lag_ref.at[0, pl.ds(row, R), :], stream.at[slot, pl.ds(0, R), :], lsem.at[slot]
        )

    lag_copy(jnp.int32(0)).start()
    acc[...] = jnp.zeros_like(acc)
    XB = pick(D, (512, 256, 128))

    def transpose(k, _):
        o = pl.multiple_of(k * XB, XB)
        xt[pl.ds(o, XB), :] = x_ref[:, pl.ds(o, XB)].T
        return 0

    lax.fori_loop(0, D // XB, transpose, 0)
    pl.semaphore_wait(barrier, len(peers))

    NB = pick(F, (512, 256, 128))

    def r1_copy(cc):
        return remote(chg.at[cc, 1 - core], r1.at[cc], r1s.at[cc], r1r.at[cc], partner)

    def change_step(i, send, last):
        cc, par = dest(i)
        row = pl.multiple_of((2 * cc + par) * R, 8)
        slot = lax.rem(i, 2)
        if not last:
            lag_copy(i + 1).start()
        lag_copy(i).wait()
        left = xt[pl.ds(row, R), :]

        def tile(n, _):
            o = pl.multiple_of(n * NB, NB)
            g = jnp.dot(left, g_ref[:, pl.ds(o, NB)], preferred_element_type=F32) * inverse
            ch = g - stream[slot, pl.ds(0, R), pl.ds(o, NB)].astype(F32)
            acc[...] += (ch * ch).reshape(R // 8, 8, NB).sum(0)
            chg[cc, par, :, pl.ds(o, NB)] = ch.astype(BF16)
            return 0

        lax.fori_loop(0, F // NB, tile, 0)
        if send:
            r1_copy(cc).start()

    def send_step(i, _):
        change_step(i, True, False)
        return 0

    def own_step(i, _):
        change_step(i, False, False)
        return 0

    lax.fori_loop(0, NC, send_step, 0)
    lax.fori_loop(NC, 2 * NC - 1, own_step, 0)
    change_step(jnp.int32(2 * NC - 1), False, True)

    def owner_at(i):
        return jnp.where(2 * t < T, T - 1 - i // 2, i // 2)

    def w_copy(i):
        h = lax.rem(i, 2)
        row = pl.multiple_of(owner_at(i) * (2 * CH) + h * CH, 8)
        return pltpu.make_async_copy(
            w_ref.at[pl.ds(row, CH), :], stream.at[h, pl.ds(0, CH), :], lsem.at[h]
        )

    w_copy(jnp.int32(0)).start()
    w_copy(jnp.int32(1)).start()

    total = jnp.sum(jnp.sum(acc[...], axis=1, keepdims=True), axis=0, keepdims=True)
    stat[0] = jnp.broadcast_to(total, (8, 128))
    stat[1] = jnp.full((8, 128), mask_ref[0].astype(F32), F32)
    stat_copies = []
    for m in range(T):
        for c in range(2):
            if m or c:
                n = 2 * m + c - 1
                stat_copies.append(remote(
                    stat, statr.at[n], sts.at[n], strr.at[n],
                    (2 * chip + (core if c == 0 else 1 - core), lax.rem(t + m, T))))
    for copy in stat_copies:
        copy.start()
    for copy in stat_copies:
        copy.wait()
    own_sq = stat[0]
    for m in range(1, T):
        own_sq = own_sq + statr[2 * m - 1, 0]
    par_sq = statr[0, 0]
    for m in range(1, T):
        par_sq = par_sq + statr[2 * m, 0]

    def rms_of(sq):
        return jnp.sqrt(sq / (D * FF) + 1e-06)

    rms_own = rms_of(own_sq)
    rms_ref[...] = rms_own
    f_own = (stat[1] * jnp.minimum(1.0, clip_level / rms_own))[0:1, 0:1]
    f_par = (statr[0, 1] * jnp.minimum(1.0, clip_level / rms_of(par_sq)))[0:1, 0:1]

    def r1_wait(cc, _):
        r1_copy(cc).wait()
        return 0

    lax.fori_loop(0, NC, r1_wait, 0)

    RB = pick(R, (64, 32, 16))

    def combine(cc, half, arrived, final):
        cols = pl.ds(half * FH, FH)

        def rows(i, _):
            rr = pl.ds(pl.multiple_of(i * RB, RB), RB)
            v = chg[cc, core, rr, cols].astype(F32) * f_own + r1[cc, rr, cols].astype(F32) * f_par
            for ref in arrived:
                v = v + ref[rr, :].astype(F32)
            if final:
                out_ref[rr, cols] = v.astype(BF16)
            else:
                chg[cc, core, rr, cols] = v.astype(BF16)
            return 0

        lax.fori_loop(0, R // RB, rows, 0)

    def half_of(cc, half):
        return chg.at[cc, core, :, pl.ds(half * FH, FH)]

    a1c, b1c, a2c, b2c = {}, {}, {}, {}

    def send_a1(k, j):
        cc = chip_at(x + k, y + j)
        combine(cc, 0, (), False)
        n = (k - 1) * NY + j
        a1c[k, j] = remote(half_of(cc, 0), a1.at[n], a1s.at[n], a1r.at[n], peer(chip_at(x + k, y)))
        a1c[k, j].start()

    def send_b1(k, j):
        cc = chip_at(x + j, y + k)
        combine(cc, 1, (), False)
        n = (k - 1) * NX + j
        b1c[k, j] = remote(half_of(cc, 1), b1.at[n], b1s.at[n], b1r.at[n], peer(chip_at(x, y + k)))
        b1c[k, j].start()

    order_a = [(k, j) for j in list(range(1, NY)) + [0] for k in range(1, NX)]
    order_b = [(k, j) for j in list(range(1, NX)) + [0] for k in range(1, NY)]
    for n in range(max(len(order_a), len(order_b))):
        if n < len(order_a):
            send_a1(*order_a[n])
        if n < len(order_b):
            send_b1(*order_b[n])

    def z_copy(owner, h):
        nxt = jnp.where(owner > t, t + 1, t - 1)
        slot = jnp.where((owner < t) & (owner == nxt), T, owner)
        return remote(
            pi.at[2 * owner + h], zr.at[2 * slot + h], zs.at[2 * owner + h], zrs.at[2 * slot + h], (dp, nxt)
        )

    def z_arrived(slot, h):
        remote(
            pi.at[h], zr.at[2 * slot + h], zs.at[h], zrs.at[2 * slot + h], (dp, lax.rem(t + 1, T))
        ).wait_recv()

    TB = pick(tok, (64, 32, 16))

    def z_add(owner, slot, h):
        z_arrived(slot, h)

        def rows(i, _):
            rr = pl.ds(pl.multiple_of(i * TB, TB), TB)
            v = pi[2 * owner + h, rr, :].astype(F32) + zr[2 * slot + h, rr, :].astype(F32)
            pi[2 * owner + h, rr, :] = v.astype(BF16)
            return 0

        lax.fori_loop(0, tok // TB, rows, 0)

    def z_relay(owner):
        for h in range(2):
            z_add(owner, owner, h)
            z_copy(owner, h).start()

    at_end = (t == 0) | (t == T - 1)

    def pi_step(i, more):
        h = lax.rem(i, 2)
        owner = owner_at(i)
        w_copy(i).wait()
        pi[2 * owner + h] = lax.dot_general(
            g_ref[...], stream[h, pl.ds(0, CH), :], (((1,), (1,)), ((), ())), preferred_element_type=F32
        ).astype(BF16)
        if more:
            w_copy(i + 2).start()

        @pl.when(at_end & (owner != t))
        def _():
            z_copy(owner, h).start()

    def pi_more(i, _):
        pi_step(i, True)
        return 0

    lax.fori_loop(0, 2 * (T - 1), pi_more, 0)

    def pi_last(i, _):
        pi_step(i, False)
        return 0

    lax.fori_loop(2 * (T - 1), 2 * T, pi_last, 0)

    for u in range(1, T - 1):
        right = T - 1 - (u - t)
        left = u - (T - 1 - t)

        @pl.when((t > 0) & (u >= t) & (right > t))
        def _():
            z_relay(right)

        @pl.when((t < T - 1) & (left >= 0) & (left < t))
        def _():
            z_relay(left)

    for j in range(1, NY):
        for k in range(1, NX):
            a1c[k, j].wait()
        cc = chip_at(x, y + j)
        combine(cc, 0, [a1.at[(k - 1) * NY + j] for k in range(1, NX)], False)
        a2c[j] = remote(half_of(cc, 0), a2.at[j - 1], a2s.at[j - 1], a2r.at[j - 1], peer(cc))
        a2c[j].start()
    for j in range(1, NX):
        for k in range(1, NY):
            b1c[k, j].wait()
        cc = chip_at(x + j, y)
        combine(cc, 1, [b1.at[(k - 1) * NX + j] for k in range(1, NY)], False)
        b2c[j] = remote(half_of(cc, 1), b2.at[j - 1], b2s.at[j - 1], b2r.at[j - 1], peer(cc))
        b2c[j].start()

    @pl.when(t > 0)
    def _():
        for h in range(2):
            z_add(t, t, h)

    @pl.when(t < T - 1)
    def _():
        for h in range(2):
            z_add(t, T, h)

    for h in range(2):
        ig_ref[:, pl.ds(h * CH, CH)] = pi[2 * t + h]
    for owner in range(T):
        @pl.when(owner != t)
        def _():
            for h in range(2):
                z_copy(owner, h).wait_send()

    for k in range(1, NX):
        a1c[k, 0].wait()
    for j in range(1, NY):
        a2c[j].wait()
    combine(chip, 0, [a1.at[(k - 1) * NY] for k in range(1, NX)] + [a2.at[j - 1] for j in range(1, NY)], True)
    for k in range(1, NY):
        b1c[k, 0].wait()
    for j in range(1, NX):
        b2c[j].wait()
    combine(chip, 1, [b1.at[(k - 1) * NX] for k in range(1, NY)] + [b2.at[j - 1] for j in range(1, NX)], True)


def body(cfg, tokens, gate_weight, up_act, hidden_cot, lag_grads, skip_mask, aggregate):
    NX, NY, T, D, FF = cfg
    NC = NX * NY
    gate = jnp.dot(tokens, gate_weight, preferred_element_type=F32)
    sig = jax.nn.sigmoid(gate)
    d_gate = (
        hidden_cot.astype(F32) * up_act.astype(F32) * sig * (1.0 + gate * (1.0 - sig))
    ).astype(BF16)
    tok, F = d_gate.shape
    R = D // (2 * NC)
    CH = D // T // 2
    FH = F // 2
    NB = pick(F, (512, 256, 128))
    nA, nB = (NX - 1) * NY, (NY - 1) * NX
    vmem = pl.BlockSpec(memory_space=pltpu.VMEM)
    hbm = pl.BlockSpec(memory_space=pl.ANY)
    dma = pltpu.SemaphoreType.DMA
    summed, input_grad, rms = pl.pallas_call(
        functools.partial(kernel, cfg),
        out_shape=(
            jax.ShapeDtypeStruct((R, F), BF16),
            jax.ShapeDtypeStruct((tok, 2 * CH), BF16),
            jax.ShapeDtypeStruct((8, 128), F32),
        ),
        in_specs=[vmem, vmem, pl.BlockSpec(memory_space=pltpu.SMEM), hbm, hbm],
        out_specs=(vmem, vmem, vmem),
        scratch_shapes=[
            pltpu.VMEM((D, tok), BF16),
            pltpu.VMEM((NC, 2, R, F), BF16),
            pltpu.VMEM((NC, R, F), BF16),
            pltpu.VMEM((nA, R, FH), BF16),
            pltpu.VMEM((NY - 1, R, FH), BF16),
            pltpu.VMEM((nB, R, FH), BF16),
            pltpu.VMEM((NX - 1, R, FH), BF16),
            pltpu.VMEM((2, max(R, CH), F), BF16),
            pltpu.VMEM((2 * T, tok, CH), BF16),
            pltpu.VMEM((2 * (T + 1), tok, CH), BF16),
            pltpu.VMEM((8, NB), F32),
            pltpu.VMEM((2, 8, 128), F32),
            pltpu.VMEM((2 * T - 1, 2, 8, 128), F32),
            dma((2,)),
            dma((NC,)), dma((NC,)),
            dma((nA,)), dma((nA,)),
            dma((NY - 1,)), dma((NY - 1,)),
            dma((nB,)), dma((nB,)),
            dma((NX - 1,)), dma((NX - 1,)),
            dma((2 * T,)), dma((2 * (T + 1),)),
            dma((2 * T - 1,)), dma((2 * T - 1,)),
        ],
        compiler_params=pltpu.CompilerParams(
            collective_id=0, has_side_effects=True, vmem_limit_bytes=67043328
        ),
    )(tokens, d_gate, skip_mask, lag_grads, gate_weight)
    return (aggregate + summed.astype(F32), input_grad, rms[0, 0:1])


def solution(mesh):
    dp, tensor = mesh.shape["dp"], mesh.shape["tensor"]

    def whole(tokens, gate_weight, *rest):
        D, FF = gate_weight.shape
        cfg = (2, dp // 4, tensor, D, FF)
        return jax.shard_map(
            functools.partial(body, cfg),
            mesh=mesh,
            in_specs=(
                P("dp", None),
                P(None, "tensor"),
                P("dp", "tensor"),
                P("dp", "tensor"),
                P("dp", None, "tensor"),
                P("dp"),
                P("dp", "tensor"),
            ),
            out_specs=(P("dp", "tensor"), P("dp", "tensor"), P("dp")),
            check_vma=False,
        )(tokens, gate_weight, *rest)

    return whole
```

```python
import functools

import jax
import jax.numpy as jnp
from jax import lax
from jax.experimental import pallas as pl
from jax.experimental.pallas import tpu as pltpu
from jax.sharding import PartitionSpec as P

MESH = pl.DeviceIdType.MESH
clip_level = 0.1
F32 = jnp.float32
BF16 = jnp.bfloat16


def pick(size, options):
    for option in options:
        if size % option == 0:
            return option
    return size


def kernel(cfg, x_ref, g_ref, mask_ref, lag_ref, w_ref, out_ref, ig_ref, rms_ref,
           xt, chg, r1, a1, a2, b1, b2, stream, pi, zr, acc, stat, statr,
           lsem, r1s, r1r, a1s, a1r, a2s, a2r, b1s, b1r, b2s, b2r, zs, zrs, sts, strr):
    NX, NY, T, D, FF = cfg
    NC = NX * NY
    tok, F = g_ref.shape
    R = chg.shape[2]
    FH = F // 2
    CH = pi.shape[2]
    inverse = 1.0 / tok
    dp = lax.axis_index("dp")
    t = lax.axis_index("tensor")
    core = lax.rem(dp, 2)
    chip = dp // 2
    x = lax.rem(chip, NX)
    y = chip // NX

    def chip_at(xx, yy):
        return lax.rem(xx, NX) + NX * lax.rem(yy, NY)

    def peer(cc):
        return (2 * cc + core, t)

    partner = (2 * chip + 1 - core, t)

    barrier = pltpu.get_barrier_semaphore()
    peers = []
    for m in range(T):
        for c in range(2):
            if m or c:
                peers.append((2 * chip + (core if c == 0 else 1 - core), lax.rem(t + m, T)))
    for k in range(1, NX):
        peers.append(peer(chip_at(x + k, y)))
    for k in range(1, NY):
        peers.append(peer(chip_at(x, y + k)))
    for p in peers:
        pl.semaphore_signal(barrier, inc=1, device_id=p, device_id_type=MESH)

    def remote(src, dst, ss, rs, dev):
        return pltpu.make_async_remote_copy(
            src_ref=src, dst_ref=dst, send_sem=ss, recv_sem=rs, device_id=dev, device_id_type=MESH
        )

    def dest(i):
        own = i // NC
        cc = lax.rem(chip + 1 + lax.rem(i, NC), NC)
        par = own * core + (1 - own) * (1 - core)
        return cc, par

    def lag_copy(i):
        cc, par = dest(i)
        row = pl.multiple_of((2 * cc + par) * R, 8)
        slot = lax.rem(i, 2)
        return pltpu.make_async_copy(
            lag_ref.at[0, pl.ds(row, R), :], stream.at[slot, pl.ds(0, R), :], lsem.at[slot]
        )

    lag_copy(jnp.int32(0)).start()
    acc[...] = jnp.zeros_like(acc)
    XB = pick(D, (512, 256, 128))

    def transpose(k, _):
        o = pl.multiple_of(k * XB, XB)
        xt[pl.ds(o, XB), :] = (x_ref[:, pl.ds(o, XB)] * inverse).astype(BF16).T
        return 0

    lax.fori_loop(0, D // XB, transpose, 0)
    pl.semaphore_wait(barrier, len(peers))

    NB = pick(F, (256, 128))

    def r1_copy(cc):
        return remote(chg.at[cc, 1 - core], r1.at[cc], r1s.at[cc], r1r.at[cc], partner)

    def change_step(i, send, last):
        cc, par = dest(i)
        row = pl.multiple_of((2 * cc + par) * R, 8)
        slot = lax.rem(i, 2)
        if not last:
            lag_copy(i + 1).start()
        lag_copy(i).wait()
        left = xt[pl.ds(row, R), :]

        def tile(n, _):
            o = pl.multiple_of(n * NB, NB)
            g = jnp.dot(left, g_ref[:, pl.ds(o, NB)], preferred_element_type=F32)
            ch = g - stream[slot, pl.ds(0, R), pl.ds(o, NB)].astype(F32)
            acc[...] += (ch * ch).reshape(R // 8, 8, NB).sum(0)
            chg[cc, par, :, pl.ds(o, NB)] = ch.astype(BF16)
            return 0

        lax.fori_loop(0, F // NB, tile, 0, unroll=True)
        if send:
            r1_copy(cc).start()

    def send_step(i, _):
        change_step(i, True, False)
        return 0

    def own_step(i, _):
        change_step(i, False, False)
        return 0

    lax.fori_loop(0, NC, send_step, 0)
    lax.fori_loop(NC, 2 * NC - 1, own_step, 0)
    change_step(jnp.int32(2 * NC - 1), False, True)

    def owner_at(i):
        return jnp.where(2 * t < T, T - 1 - i // 2, i // 2)

    def w_copy(i):
        h = lax.rem(i, 2)
        row = pl.multiple_of(owner_at(i) * (2 * CH) + h * CH, 8)
        return pltpu.make_async_copy(
            w_ref.at[pl.ds(row, CH), :], stream.at[h, pl.ds(0, CH), :], lsem.at[h]
        )

    w_copy(jnp.int32(0)).start()
    w_copy(jnp.int32(1)).start()

    total = jnp.sum(jnp.sum(acc[...], axis=1, keepdims=True), axis=0, keepdims=True)
    stat[0] = jnp.broadcast_to(total, (8, 128))
    stat[1] = jnp.full((8, 128), mask_ref[0].astype(F32), F32)
    stat_copies = []
    for m in range(T):
        for c in range(2):
            if m or c:
                n = 2 * m + c - 1
                stat_copies.append(remote(
                    stat, statr.at[n], sts.at[n], strr.at[n],
                    (2 * chip + (core if c == 0 else 1 - core), lax.rem(t + m, T))))
    for copy in stat_copies:
        copy.start()
    for copy in stat_copies:
        copy.wait()
    own_sq = stat[0]
    for m in range(1, T):
        own_sq = own_sq + statr[2 * m - 1, 0]
    par_sq = statr[0, 0]
    for m in range(1, T):
        par_sq = par_sq + statr[2 * m, 0]

    def rms_of(sq):
        return jnp.sqrt(sq / (D * FF) + 1e-06)

    rms_own = rms_of(own_sq)
    rms_ref[...] = rms_own
    f_own = (stat[1] * jnp.minimum(1.0, clip_level / rms_own))[0:1, 0:1]
    f_par = (statr[0, 1] * jnp.minimum(1.0, clip_level / rms_of(par_sq)))[0:1, 0:1]

    def r1_wait(cc, _):
        r1_copy(cc).wait()
        return 0

    lax.fori_loop(0, NC, r1_wait, 0)

    RB = pick(R, (64, 32, 16))

    def combine(cc, half, arrived, final):
        cols = pl.ds(half * FH, FH)

        def rows(i, _):
            rr = pl.ds(pl.multiple_of(i * RB, RB), RB)
            v = chg[cc, core, rr, cols].astype(F32) * f_own + r1[cc, rr, cols].astype(F32) * f_par
            for ref in arrived:
                v = v + ref[rr, :].astype(F32)
            if final:
                out_ref[rr, cols] = v.astype(BF16)
            else:
                chg[cc, core, rr, cols] = v.astype(BF16)
            return 0

        lax.fori_loop(0, R // RB, rows, 0)

    def half_of(cc, half):
        return chg.at[cc, core, :, pl.ds(half * FH, FH)]

    a1c, b1c, a2c, b2c = {}, {}, {}, {}

    def send_a1(k, j):
        cc = chip_at(x + k, y + j)
        combine(cc, 0, (), False)
        n = (k - 1) * NY + j
        a1c[k, j] = remote(half_of(cc, 0), a1.at[n], a1s.at[n], a1r.at[n], peer(chip_at(x + k, y)))
        a1c[k, j].start()

    def send_b1(k, j):
        cc = chip_at(x + j, y + k)
        combine(cc, 1, (), False)
        n = (k - 1) * NX + j
        b1c[k, j] = remote(half_of(cc, 1), b1.at[n], b1s.at[n], b1r.at[n], peer(chip_at(x, y + k)))
        b1c[k, j].start()

    for j in range(1, NY):
        for k in range(1, NX):
            send_a1(k, j)
    for j in range(1, NX):
        for k in range(1, NY):
            send_b1(k, j)

    def z_copy(owner, h):
        nxt = jnp.where(owner > t, t + 1, t - 1)
        slot = jnp.where((owner < t) & (owner == nxt), T, owner)
        return remote(
            pi.at[2 * owner + h], zr.at[2 * slot + h], zs.at[2 * owner + h], zrs.at[2 * slot + h], (dp, nxt)
        )

    def z_arrived(slot, h):
        remote(
            pi.at[h], zr.at[2 * slot + h], zs.at[h], zrs.at[2 * slot + h], (dp, lax.rem(t + 1, T))
        ).wait_recv()

    TB = pick(tok, (64, 32, 16))

    def z_add(owner, slot, h):
        z_arrived(slot, h)

        def rows(i, _):
            rr = pl.ds(pl.multiple_of(i * TB, TB), TB)
            v = pi[2 * owner + h, rr, :].astype(F32) + zr[2 * slot + h, rr, :].astype(F32)
            pi[2 * owner + h, rr, :] = v.astype(BF16)
            return 0

        lax.fori_loop(0, tok // TB, rows, 0)

    def z_relay(owner):
        for h in range(2):
            z_add(owner, owner, h)
            z_copy(owner, h).start()

    at_end = (t == 0) | (t == T - 1)

    def pi_step(i, more):
        h = lax.rem(i, 2)
        owner = owner_at(i)
        w_copy(i).wait()
        pi[2 * owner + h] = lax.dot_general(
            g_ref[...], stream[h, pl.ds(0, CH), :], (((1,), (1,)), ((), ())), preferred_element_type=F32
        ).astype(BF16)
        if more:
            w_copy(i + 2).start()

        @pl.when(at_end & (owner != t))
        def _():
            z_copy(owner, h).start()

    def pi_more(i, _):
        pi_step(i, True)
        return 0

    lax.fori_loop(0, 2 * (T - 1), pi_more, 0)

    def pi_last(i, _):
        pi_step(i, False)
        return 0

    lax.fori_loop(2 * (T - 1), 2 * T, pi_last, 0)

    for k in range(1, NX):
        send_a1(k, 0)
    for k in range(1, NY):
        send_b1(k, 0)

    def z_step(u):
        right = T - 1 - (u - t)
        left = u - (T - 1 - t)

        @pl.when((t > 0) & (u >= t) & (right > t))
        def _():
            z_relay(right)

        @pl.when((t < T - 1) & (left >= 0) & (left < t))
        def _():
            z_relay(left)

    z_step(1)

    for j in range(1, NY):
        for k in range(1, NX):
            a1c[k, j].wait()
        cc = chip_at(x, y + j)
        combine(cc, 0, [a1.at[(k - 1) * NY + j] for k in range(1, NX)], False)
        a2c[j] = remote(half_of(cc, 0), a2.at[j - 1], a2s.at[j - 1], a2r.at[j - 1], peer(cc))
        a2c[j].start()
    for j in range(1, NX):
        for k in range(1, NY):
            b1c[k, j].wait()
        cc = chip_at(x + j, y)
        combine(cc, 1, [b1.at[(k - 1) * NX + j] for k in range(1, NY)], False)
        b2c[j] = remote(half_of(cc, 1), b2.at[j - 1], b2s.at[j - 1], b2r.at[j - 1], peer(cc))
        b2c[j].start()

    for u in range(2, T - 1):
        z_step(u)

    @pl.when(t > 0)
    def _():
        for h in range(2):
            z_add(t, t, h)

    @pl.when(t < T - 1)
    def _():
        for h in range(2):
            z_add(t, T, h)

    for h in range(2):
        ig_ref[:, pl.ds(h * CH, CH)] = pi[2 * t + h]
    for owner in range(T):
        @pl.when(owner != t)
        def _():
            for h in range(2):
                z_copy(owner, h).wait_send()

    for k in range(1, NX):
        a1c[k, 0].wait()
    for j in range(1, NY):
        a2c[j].wait()
    combine(chip, 0, [a1.at[(k - 1) * NY] for k in range(1, NX)] + [a2.at[j - 1] for j in range(1, NY)], True)
    for k in range(1, NY):
        b1c[k, 0].wait()
    for j in range(1, NX):
        b2c[j].wait()
    combine(chip, 1, [b1.at[(k - 1) * NX] for k in range(1, NY)] + [b2.at[j - 1] for j in range(1, NX)], True)


def body(cfg, tokens, gate_weight, up_act, hidden_cot, lag_grads, skip_mask, aggregate):
    NX, NY, T, D, FF = cfg
    NC = NX * NY
    gate = jnp.dot(tokens, gate_weight, preferred_element_type=F32)
    sig = jax.nn.sigmoid(gate)
    d_gate = (
        hidden_cot.astype(F32) * up_act.astype(F32) * sig * (1.0 + gate * (1.0 - sig))
    ).astype(BF16)
    tok, F = d_gate.shape
    R = D // (2 * NC)
    CH = D // T // 2
    FH = F // 2
    NB = pick(F, (256, 128))
    nA, nB = (NX - 1) * NY, (NY - 1) * NX
    vmem = pl.BlockSpec(memory_space=pltpu.VMEM)
    hbm = pl.BlockSpec(memory_space=pl.ANY)
    dma = pltpu.SemaphoreType.DMA
    summed, input_grad, rms = pl.pallas_call(
        functools.partial(kernel, cfg),
        out_shape=(
            jax.ShapeDtypeStruct((R, F), BF16),
            jax.ShapeDtypeStruct((tok, 2 * CH), BF16),
            jax.ShapeDtypeStruct((8, 128), F32),
        ),
        in_specs=[vmem, vmem, pl.BlockSpec(memory_space=pltpu.SMEM), hbm, hbm],
        out_specs=(vmem, vmem, vmem),
        scratch_shapes=[
            pltpu.VMEM((D, tok), BF16),
            pltpu.VMEM((NC, 2, R, F), BF16),
            pltpu.VMEM((NC, R, F), BF16),
            pltpu.VMEM((nA, R, FH), BF16),
            pltpu.VMEM((NY - 1, R, FH), BF16),
            pltpu.VMEM((nB, R, FH), BF16),
            pltpu.VMEM((NX - 1, R, FH), BF16),
            pltpu.VMEM((2, max(R, CH), F), BF16),
            pltpu.VMEM((2 * T, tok, CH), BF16),
            pltpu.VMEM((2 * (T + 1), tok, CH), BF16),
            pltpu.VMEM((8, NB), F32),
            pltpu.VMEM((2, 8, 128), F32),
            pltpu.VMEM((2 * T - 1, 2, 8, 128), F32),
            dma((2,)),
            dma((NC,)), dma((NC,)),
            dma((nA,)), dma((nA,)),
            dma((NY - 1,)), dma((NY - 1,)),
            dma((nB,)), dma((nB,)),
            dma((NX - 1,)), dma((NX - 1,)),
            dma((2 * T,)), dma((2 * (T + 1),)),
            dma((2 * T - 1,)), dma((2 * T - 1,)),
        ],
        compiler_params=pltpu.CompilerParams(
            collective_id=0, has_side_effects=True, vmem_limit_bytes=67043328
        ),
    )(tokens, d_gate, skip_mask, lag_grads, gate_weight)
    return (aggregate + summed.astype(F32), input_grad, rms[0, 0:1])


def solution(mesh):
    dp, tensor = mesh.shape["dp"], mesh.shape["tensor"]

    def whole(tokens, gate_weight, *rest):
        D, FF = gate_weight.shape
        cfg = (2, dp // 4, tensor, D, FF)
        return jax.shard_map(
            functools.partial(body, cfg),
            mesh=mesh,
            in_specs=(
                P("dp", None),
                P(None, "tensor"),
                P("dp", "tensor"),
                P("dp", "tensor"),
                P("dp", None, "tensor"),
                P("dp"),
                P("dp", "tensor"),
            ),
            out_specs=(P("dp", "tensor"), P("dp", "tensor"), P("dp")),
            check_vma=False,
        )(tokens, gate_weight, *rest)

    return whole
```
